32 devices in a mesh: parts: 2 (over y), tm: 16 (over z, x, core).
Axes of the slice: x: 2, y: 2, z: 4, core: 2. Of those that a mesh axis runs over, the one named last changes fastest.
Arguments:
- frames: bfloat16 [2048, 2048], P('tm', 'parts'), parts along dimension 1, may hold values from -6 to 6
- levels: int32 [2048], P(('parts', 'tm')), parts along dimension 0, may hold values from 0 to 15
- initial_state: float32 [256], P('parts'), parts along dimension 0, may hold values from -6 to 6
- transitions: float32 [16, 128, 128], replicated, may hold values from -1 to 1
- gain: bfloat16 [128, 128], replicated, may hold values from -1 to 1
- pixel_mode: int32 [2048], replicated, may hold values from 0 to 127
- pixel_weight: bfloat16 [2048], replicated, may hold values from 0.099609375 to 0.5
Outputs:
- estimates: float32 [2048, 128], P(('parts', 'tm')), parts along dimension 0
The draws below stay inside these ranges and needn't reach their ends.
There are 2 independent parts, one for each index of `parts`. The reference program is written for one: setup_inputs(seed, part) draws one part's arguments, and reference() takes and returns one part's arrays. A program takes and returns all parts, laid end to end along the dimension named above; an argument that names none is the same for every part. Nothing has to cross between parts.
All inputs are finite; a program needn't handle non-finite values.
Results may differ from the reference program's by a relative error of at most 0.0026.
Values may be sent and summed in bfloat16 or wider, within the bound.
A program may use at most 128 MiB of HBM per device.

```python
import math
import jax
import jax.numpy as jnp
from jax import lax

MODAL_DIMENSION = 128
PIX = 2048
LEVELS = 16
FRAMES = 1024


def mode_traits(key):
    modes = MODAL_DIMENSION // 2
    perm = jax.random.permutation(jax.random.fold_in(key, 1), modes)
    slow_count = modes // 2
    lagging_mode_choice = perm < slow_count
    keep = jax.random.uniform(jax.random.fold_in(key, 2), (modes,), jnp.float32, 0.3, 0.8)
    slow_rate = jnp.exp(jnp.log(keep) / FRAMES)
    fast_rate = jax.random.uniform(jax.random.fold_in(key, 3), (modes,), jnp.float32, 0.95, 0.975)
    capture_frequency = jnp.where(lagging_mode_choice, slow_rate, fast_rate)
    base = jax.random.uniform(jax.random.fold_in(key, 4), (modes,), jnp.float32, 0.05, 1.5)
    return (lagging_mode_choice, capture_frequency, base)


def draw_levels(key, part):
    holds = FRAMES // 16
    values = jax.random.randint(jax.random.fold_in(key, 21), (holds,), 1, LEVELS)
    values = values.at[0].set(LEVELS - 1)
    plan = jnp.repeat(values, 16)
    spots = jax.random.randint(jax.random.fold_in(key, 22), (4,), 0, FRAMES)
    plan = plan.at[spots].set(0)
    return plan.astype(jnp.int32)


def draw_transitions(key, part):
    lagging_mode_choice, capture_frequency, base = mode_traits(key)
    tension = jax.random.uniform(jax.random.fold_in(key, 5), (LEVELS,), jnp.float32, 0.7, 1.3)
    image_count_per_group = jax.random.uniform(jax.random.fold_in(key, 6), (MODAL_DIMENSION // 2,), jnp.float32, 0.5, 0.8)
    omega = base[None, :] * jnp.sqrt(tension)[:, None]
    tier_indices = jnp.arange(LEVELS)
    neighborhood_extent = capture_frequency[None, :] * jnp.where((tier_indices[:, None] == 0) & lagging_mode_choice[None, :], image_count_per_group[None, :], 1.0)
    cosine = neighborhood_extent * jnp.cos(omega)
    sine = neighborhood_extent * jnp.sin(omega)
    rows = jnp.arange(MODAL_DIMENSION)
    row_mode = rows // 2
    row_part = rows % 2
    partner = rows + 1 - 2 * row_part
    same = row_mode[:, None] == row_mode[None, :]
    cos_rows = cosine[:, row_mode][:, :, None]
    sin_rows = sine[:, row_mode][:, :, None]
    block = jnp.where(row_part[:, None] == row_part[None, :], cos_rows, jnp.where(row_part[:, None] < row_part[None, :], sin_rows, -sin_rows))
    rotation = jnp.where(same[None, :, :], block, 0.0)
    diag_val = cosine[:, row_mode]
    off_val = jnp.where(row_part[None, :] == 0, sine[:, row_mode], -sine[:, row_mode])
    amp = jnp.sqrt(jnp.float32(0.2) / (jnp.float32(MODAL_DIMENSION) * jnp.float32(FRAMES)))
    noise = jax.random.uniform(jax.random.fold_in(key, 7), (LEVELS, MODAL_DIMENSION, MODAL_DIMENSION), jnp.float32, -1.0, 1.0)
    upper = rows[:, None] < rows[None, :]
    lower = rows[:, None] > rows[None, :]
    skew = amp * jnp.where(upper[None, :, :], noise, jnp.where(lower[None, :, :], -jnp.transpose(noise, (0, 2, 1)), 0.0))
    skew_partner = jnp.take(skew, partner, axis=1)
    table = rotation + diag_val[:, :, None] * skew + off_val[:, :, None] * skew_partner
    return table.astype(jnp.float32)


def draw_gain(key, part):
    lagging_mode_choice, capture_frequency, base = mode_traits(key)
    row_rate = capture_frequency[jnp.arange(MODAL_DIMENSION) // 2]
    scale = jnp.sqrt(1.0 - row_rate * row_rate)
    raw = jax.random.normal(jax.random.fold_in(key, 8), (MODAL_DIMENSION, MODAL_DIMENSION), jnp.float32)
    return (scale[:, None] * raw / jnp.sqrt(jnp.float32(MODAL_DIMENSION))).astype(jnp.bfloat16)


def with_ends(entries, key, least, high):
    longest = entries.shape.index(max(entries.shape))
    spots = []
    for shift in (0, 1):
        where = [jax.random.randint(jax.random.fold_in(key, axis), (), 0, length) for axis, length in enumerate(entries.shape)]
        where[longest] = (where[longest] + shift) % entries.shape[longest]
        spots.append(tuple(where))
    return entries.at[spots[0]].set(least).at[spots[1]].set(high)


def shard_levels(key, dims, pieces, smallest, high):
    def one(dim, parts):
        steps = jax.random.uniform(jax.random.fold_in(jax.random.fold_in(key, 6), dim), (parts,), jnp.float32, smallest / len(pieces), high / len(pieces))
        return jnp.repeat(jnp.exp(steps), dims[dim] // parts).reshape((-1,) + (1,) * (len(dims) - dim - 1))

    level = one(*pieces[0])
    for cut in pieces[1:]:
        level = level * one(*cut)
    return level


def normal_values(own_key, shape, scale, bound, pieces=(), kind=jnp.bfloat16):
    result = jax.random.normal(own_key, shape, jnp.float32) * scale
    if len(pieces) > 0:
        result = shard_levels(own_key, shape, pieces, -0.22, 0.18) * result
    return jnp.clip(result, min=-bound, max=bound).astype(kind)


def setup_inputs(seed: int = 0, part: int = 0) -> dict:
    arg_keys = jax.random.split(jax.random.key(seed), 8)
    own_keys = jax.random.split(jax.random.fold_in(arg_keys[7], part), 8)
    frames = normal_values(own_keys[0], (PIX, FRAMES), 1.0, 6.0, ((0, 16),))
    levels = draw_levels(jax.random.fold_in(jax.random.fold_in(arg_keys[7], part), 71), part)
    initial_state = normal_values(own_keys[2], (MODAL_DIMENSION,), 1.0, 6.0, (), jnp.float32)
    transitions = draw_transitions(jax.random.fold_in(arg_keys[7], 71), part)
    gain = draw_gain(jax.random.fold_in(arg_keys[7], 71), part)
    pixel_mode = with_ends(jax.random.randint(arg_keys[5], (PIX,), 0, MODAL_DIMENSION), jax.random.fold_in(arg_keys[5], 1), 0, MODAL_DIMENSION - 1).astype(jnp.int32)
    pixel_weight = jnp.clip(jnp.exp(jax.random.uniform(arg_keys[6], (PIX,), jnp.float32, math.log(0.099609375), math.log(0.5))), 0.099609375, 0.5).astype(jnp.bfloat16)
    return {"frames": frames, "levels": levels, "initial_state": initial_state, "transitions": transitions, "gain": gain, "pixel_mode": pixel_mode, "pixel_weight": pixel_weight}


def reference(frames, levels, initial_state, transitions, gain, pixel_mode, pixel_weight):
    channels = jnp.arange(MODAL_DIMENSION, dtype=jnp.int32)
    projector = jnp.where(pixel_mode[None, :] == channels[:, None], pixel_weight[None, :], jnp.zeros((), jnp.bfloat16))
    measured = lax.dot_general(frames, projector, (((0,), (1,)), ((), ())), preferred_element_type=jnp.float32).astype(jnp.bfloat16)
    drive = lax.dot_general(measured, gain, (((1,), (1,)), ((), ())), preferred_element_type=jnp.float32)

    def advance(carried, inputs):
        tension, push = inputs
        moved = jnp.dot(transitions[tension], carried, precision=lax.Precision.HIGHEST) + push
        return moved, moved

    _, estimates = lax.scan(advance, initial_state, (levels, drive))
    return estimates
```

```python
import functools

import jax
import jax.numpy as jnp
from jax import lax
from jax.experimental import pallas as pl
from jax.experimental.pallas import tpu as pltpu
from jax.sharding import PartitionSpec as P

MESH = pl.DeviceIdType.MESH
F32 = jnp.float32
BF16 = jnp.bfloat16
STEPS = 8


def halves(x):
    high = x.astype(BF16)
    return high, (x - high.astype(F32)).astype(BF16)


def left_pair(x):
    high, low = halves(x)
    return jnp.concatenate([high, low], axis=1)


def right_pair(y):
    pair = left_pair(y)
    return jnp.concatenate([pair, pair], axis=0)


def joined(pair):
    return pair[:, : pair.shape[1] // 2] + pair[:, pair.shape[1] // 2 :]


def product(x, y):
    return joined(jnp.dot(left_pair(x), right_pair(y), preferred_element_type=F32))


def diagonal(size):
    return lax.broadcasted_iota(jnp.int32, (size, size), 0) == lax.broadcasted_iota(
        jnp.int32, (size, size), 1
    )


def to_column(eye, row):
    return jnp.sum(jnp.where(eye, row, 0.0), axis=1, keepdims=True)


def to_row(eye, column):
    return jnp.sum(jnp.where(eye, column, 0.0), axis=0, keepdims=True)


def row_step(eye, matrix, row, push):
    return jnp.sum(matrix * row + jnp.where(eye, push, 0.0), axis=1, keepdims=True)


def column_step(flipped, column, push):
    return jnp.sum(flipped * column, axis=0, keepdims=True) + push


def maps_kernel(levels, table, flipped, prefix, heads, ends, total, pairs):
    count = levels.shape[0] // STEPS
    for level in range(table.shape[0]):
        turned = table[level].T
        flipped[level] = turned
        pairs[level] = right_pair(turned)
    for chunk in range(count):
        prefix[chunk * STEPS] = flipped[levels[chunk * STEPS]]
    for step in range(1, STEPS):
        for chunk in range(count):
            t = chunk * STEPS + step
            prefix[t] = joined(
                jnp.dot(left_pair(prefix[t - 1]), pairs[levels[t]], preferred_element_type=F32)
            )
    spans = [prefix[chunk * STEPS + STEPS - 1] for chunk in range(count)]
    for chunk in range(count):
        ends[chunk] = spans[chunk].T if chunk % 2 else spans[chunk]
    width = 1
    while width < count:
        for chunk in range(count):
            if chunk & width:
                base = (chunk // width) * width - 1
                spans[chunk] = product(spans[base], spans[chunk])
        width *= 2
    for chunk in range(count - 1):
        heads[chunk] = spans[chunk].T
    total[0] = spans[count - 1]
    total[1] = spans[count - 1].T


def exchange_kernel(n, group, frames, total, regrouped, maps, own_sem, send_sem, recv_sem, msend_sem, mrecv_sem):
    me = lax.axis_index("tm")
    span = regrouped.shape[1]
    barrier = pltpu.get_barrier_semaphore()

    @pl.loop(1, n)
    def _(away):
        pl.semaphore_signal(barrier, inc=1, device_id={"tm": lax.rem(me + away, n)}, device_id_type=MESH)

    home = (me // group) * group
    place = lax.rem(me, group)
    own = pltpu.make_async_copy(
        frames.at[pl.ds(pl.multiple_of(me * span, span), span)], regrouped.at[me], own_sem.at[0]
    )
    own.start()
    kept = pltpu.make_async_copy(total.at[lax.rem(place, 2)], maps.at[place], own_sem.at[1])
    kept.start()
    pl.semaphore_wait(barrier, n - 1)

    def piece(away):
        target = lax.rem(me + away, n)
        return pltpu.make_async_remote_copy(
            src_ref=frames.at[pl.ds(pl.multiple_of(target * span, span), span)],
            dst_ref=regrouped.at[me],
            send_sem=send_sem.at[away],
            recv_sem=recv_sem.at[away],
            device_id={"tm": target},
            device_id_type=MESH,
        )

    def shared(away):
        return pltpu.make_async_remote_copy(
            src_ref=total.at[lax.rem(place, 2)],
            dst_ref=maps.at[place],
            send_sem=msend_sem.at[away],
            recv_sem=mrecv_sem.at[away],
            device_id={"tm": home + lax.rem(place + away, group)},
            device_id_type=MESH,
        )

    @pl.loop(1, n)
    def _(away):
        piece(away).start()

    @pl.loop(1, group)
    def _(away):
        shared(away).start()

    own.wait()
    kept.wait()

    @pl.loop(1, n)
    def _(away):
        piece(away).wait()

    @pl.loop(1, group)
    def _(away):
        shared(away).wait()


def local_kernel(levels, regrouped, modes, weights, gain, table, flipped, ends, maps, local, chunk_ends, whole):
    n, frames, pixels = regrouped.shape
    states = gain.shape[0]
    eye = diagonal(states)
    channels = lax.broadcasted_iota(jnp.int32, (states, pixels), 0)
    measured = jnp.zeros((frames, states), F32)
    for k in range(n):
        projector = jnp.where(modes[k : k + 1] == channels, weights[k : k + 1].astype(F32), 0.0)
        measured += lax.dot_general(
            regrouped[k], projector.astype(BF16), (((1,), (1,)), ((), ())), preferred_element_type=F32
        )
    local[...] = lax.dot_general(
        measured.astype(BF16), gain[...], (((1,), (1,)), ((), ())), preferred_element_type=F32
    )
    count = frames // STEPS
    held = [to_column(eye, local[c * STEPS : c * STEPS + 1]) for c in range(count)]
    for step in range(1, STEPS):
        for c in range(count):
            t = c * STEPS + step
            push = local[t : t + 1]
            if step % 2:
                held[c] = column_step(flipped[levels[t]], held[c], push)
                local[t : t + 1] = held[c]
            else:
                held[c] = row_step(eye, table[levels[t]], held[c], push)
                local[t : t + 1] = to_row(eye, held[c])
    carried = local[STEPS - 1 : STEPS]
    chunk_ends[0:1] = carried
    for c in range(1, count):
        push = local[c * STEPS + STEPS - 1 : c * STEPS + STEPS]
        if c % 2:
            carried = row_step(eye, ends[c], carried, push)
            chunk_ends[c : c + 1] = to_row(eye, carried)
        else:
            carried = column_step(ends[c], carried, push)
            chunk_ends[c : c + 1] = carried
    group = maps.shape[0]
    chain = maps[0].T
    for k in range(1, group):
        chain = product(maps[k] if k % 2 else maps[k].T, chain)
    whole[...] = chain


def chain_kernel(n, group, shift, maps, whole, start, incoming, shifts, arrived, leaving, send_sem, recv_sem, hop_send, hop_recv):
    me = lax.axis_index("tm")
    place = lax.rem(me, group)
    home = me - place
    states = whole.shape[0]
    eye = diagonal(states)
    has_next = me + group < n
    has_last = me >= group
    barrier = pltpu.get_barrier_semaphore()
    for away in range(1, group):
        pl.semaphore_signal(
            barrier, inc=1, device_id={"tm": home + lax.rem(place + away, group)}, device_id_type=MESH
        )

    @pl.when(has_last)
    def _():
        pl.semaphore_signal(barrier, inc=1, device_id={"tm": me - group}, device_id_type=MESH)

    shifts[place] = shift[...]
    pl.semaphore_wait(barrier, jnp.where(has_next, group, group - 1))

    def shared(away):
        return pltpu.make_async_remote_copy(
            src_ref=shift,
            dst_ref=shifts.at[place],
            send_sem=send_sem.at[away],
            recv_sem=recv_sem.at[away],
            device_id={"tm": home + lax.rem(place + away, group)},
            device_id_type=MESH,
        )

    for away in range(1, group):
        shared(away).start()
    for away in range(1, group):
        shared(away).wait()
    moved = shifts[0, 0:1]
    for k in range(1, group):
        push = shifts[k, 0:1]
        moved = row_step(eye, maps[k], moved, push) if k % 2 else column_step(maps[k], moved, push)
    offset = moved if group % 2 else to_row(eye, moved)

    hop = pltpu.make_async_remote_copy(
        src_ref=leaving,
        dst_ref=arrived,
        send_sem=hop_send.at[0],
        recv_sem=hop_recv.at[0],
        device_id={"tm": lax.rem(me + group, n)},
        device_id_type=MESH,
    )

    @pl.when(has_last)
    def _():
        hop.wait_recv()

    @pl.when(jnp.logical_not(has_last))
    def _():
        arrived[...] = jnp.broadcast_to(start[...], arrived.shape)

    entry = arrived[0:1]

    @pl.when(has_next)
    def _():
        leaving[...] = jnp.broadcast_to(
            to_row(eye, row_step(eye, whole[...], entry, offset)), leaving.shape
        )
        hop.start()

    inside = entry
    column = to_column(eye, entry)
    for k in range(group - 1):
        push = shifts[k, 0:1]
        if k % 2:
            column = row_step(eye, maps[k], row, push)
            after = to_row(eye, column)
        else:
            row = column_step(maps[k], column, push)
            after = row
        inside = jnp.where(place == k + 1, after, inside)
    incoming[...] = inside

    @pl.when(has_next)
    def _():
        hop.wait_send()


def finish_kernel(incoming, heads, chunk_ends, prefix, local, out):
    frames, states = local.shape
    eye = diagonal(states)
    entry = incoming[...]
    for c in range(frames // STEPS):
        if c:
            column = row_step(eye, heads[c - 1], entry, chunk_ends[c - 1 : c])
        else:
            column = to_column(eye, entry)
        for step in range(STEPS):
            t = c * STEPS + step
            out[t : t + 1] = column_step(prefix[t], column, local[t : t + 1])


VMEM = pl.BlockSpec(memory_space=pltpu.VMEM)
SMEM = pl.BlockSpec(memory_space=pltpu.SMEM)
ANY = pl.BlockSpec(memory_space=pl.ANY)
LIMIT = 48 * 1024 * 1024


def shape(*dims, dtype=F32):
    return jax.ShapeDtypeStruct(dims, dtype)


def shards(n, frames, levels, initial_state, transitions, gain, pixel_mode, pixel_weight):
    group = 4
    while n % group:
        group //= 2
    span = levels.shape[0]
    depth, states = transitions.shape[0], transitions.shape[1]
    pixels = frames.shape[0]
    count = span // STEPS
    plain = pltpu.CompilerParams(vmem_limit_bytes=LIMIT)
    flipped, prefix, heads, ends, total = pl.pallas_call(
        maps_kernel,
        out_shape=(
            shape(depth, states, states),
            shape(span, states, states),
            shape(count - 1, states, states),
            shape(count, states, states),
            shape(2, states, states),
        ),
        in_specs=[SMEM, VMEM],
        out_specs=(VMEM,) * 5,
        scratch_shapes=[pltpu.VMEM((depth, 2 * states, 2 * states), BF16)],
        compiler_params=plain,
        name="maps",
    )(levels, transitions)
    regrouped, maps = pl.pallas_call(
        functools.partial(exchange_kernel, n, group),
        out_shape=(shape(n, span, pixels, dtype=BF16), shape(group, states, states)),
        in_specs=[ANY, ANY],
        out_specs=(ANY, ANY),
        scratch_shapes=[
            pltpu.SemaphoreType.DMA((2,)),
            pltpu.SemaphoreType.DMA((n,)),
            pltpu.SemaphoreType.DMA((n,)),
            pltpu.SemaphoreType.DMA((group,)),
            pltpu.SemaphoreType.DMA((group,)),
        ],
        compiler_params=pltpu.CompilerParams(collective_id=0, has_side_effects=True),
        name="exchange",
    )(frames.T, total)
    local, chunk_ends, whole = pl.pallas_call(
        local_kernel,
        out_shape=(shape(span, states), shape(count, states), shape(states, states)),
        in_specs=[SMEM] + [VMEM] * 8,
        out_specs=(VMEM,) * 3,
        compiler_params=plain,
        name="local",
    )(
        levels,
        regrouped,
        pixel_mode.reshape(n, pixels),
        pixel_weight.reshape(n, pixels),
        gain,
        transitions,
        flipped,
        ends,
        maps,
    )
    shift = jnp.broadcast_to(chunk_ends[count - 1 :], (8, states))
    incoming = pl.pallas_call(
        functools.partial(chain_kernel, n, group),
        out_shape=shape(1, states),
        in_specs=[VMEM] * 4,
        out_specs=VMEM,
        scratch_shapes=[
            pltpu.VMEM((group, 8, states), F32),
            pltpu.VMEM((8, states), F32),
            pltpu.VMEM((8, states), F32),
            pltpu.SemaphoreType.DMA((group,)),
            pltpu.SemaphoreType.DMA((group,)),
            pltpu.SemaphoreType.DMA((1,)),
            pltpu.SemaphoreType.DMA((1,)),
        ],
        compiler_params=pltpu.CompilerParams(collective_id=1, has_side_effects=True),
        name="chain",
    )(shift, maps, whole, initial_state.reshape(1, states))
    return pl.pallas_call(
        finish_kernel,
        out_shape=shape(span, states),
        in_specs=[VMEM] * 5,
        out_specs=VMEM,
        compiler_params=plain,
        name="finish",
    )(incoming, heads, chunk_ends, prefix, local)


def solution(mesh):
    in_specs = (P("tm", "parts"), P(("parts", "tm")), P("parts"), P(), P(), P(), P())
    out_specs = P(("parts", "tm"), None)
    return jax.shard_map(
        functools.partial(shards, mesh.shape["tm"]),
        mesh=mesh,
        in_specs=in_specs,
        out_specs=out_specs,
        check_vma=False,
    )
```

```python
import functools

import jax
import jax.numpy as jnp
from jax import lax
from jax.experimental import pallas as pl
from jax.experimental.pallas import tpu as pltpu
from jax.sharding import PartitionSpec as P

MESH = pl.DeviceIdType.MESH
F32 = jnp.float32
BF16 = jnp.bfloat16
STEPS = 8


def halves(x):
    high = x.astype(BF16)
    return high, (x - high.astype(F32)).astype(BF16)


def left_pair(x):
    high, low = halves(x)
    return jnp.concatenate([high, low], axis=1)


def right_pair(y):
    pair = left_pair(y)
    return jnp.concatenate([pair, pair], axis=0)


def joined(pair):
    return pair[:, : pair.shape[1] // 2] + pair[:, pair.shape[1] // 2 :]


def product(x, y):
    return joined(jnp.dot(left_pair(x), right_pair(y), preferred_element_type=F32))


def diagonal(size):
    return lax.broadcasted_iota(jnp.int32, (size, size), 0) == lax.broadcasted_iota(
        jnp.int32, (size, size), 1
    )


def to_column(eye, row):
    return jnp.sum(jnp.where(eye, row, 0.0), axis=1, keepdims=True)


def to_row(eye, column):
    return jnp.sum(jnp.where(eye, column, 0.0), axis=0, keepdims=True)


def row_step(eye, matrix, row, push):
    return jnp.sum(matrix * row + jnp.where(eye, push, 0.0), axis=1, keepdims=True)


def column_step(flipped, column, push):
    return jnp.sum(flipped * column, axis=0, keepdims=True) + push


def fused_kernel(
    n, group,
    levels, frames_in, table_in, gain_in, modes_in, weights_in, start_in,
    out,
    raw, turned, regrouped, table, flipped, pairs, prefix, heads, ends, total, maps, whole,
    gain, modes, weights, start, projector, local, chunk_ends, shift, shifts, arrived, leaving,
    load_sem, own_sem, send_sem, recv_sem, msend_sem, mrecv_sem, csend_sem, crecv_sem, hop_send, hop_recv,
):
    me = lax.axis_index("tm")
    place = lax.rem(me, group)
    home = me - place
    has_next = me + group < n
    has_last = me >= group
    span = out.shape[0]
    states = gain.shape[0]
    pixels = raw.shape[0]
    count = span // STEPS
    loads = [
        pltpu.make_async_copy(source, target, load_sem.at[i])
        for i, (source, target) in enumerate(
            [(frames_in, raw), (table_in, table), (gain_in, gain), (modes_in, modes), (weights_in, weights), (start_in, start)]
        )
    ]
    for load in loads:
        load.start()
    barrier = pltpu.get_barrier_semaphore()

    @pl.loop(1, n)
    def _(away):
        pl.semaphore_signal(barrier, inc=1, device_id={"tm": lax.rem(me + away, n)}, device_id_type=MESH)

    loads[0].wait()
    for block in range(0, n * span, 128):
        turned[block : block + 128] = raw[:, block : block + 128].T
    pl.semaphore_wait(barrier, n - 1)

    def piece(away):
        target = lax.rem(me + away, n)
        return pltpu.make_async_remote_copy(
            src_ref=turned.at[pl.ds(pl.multiple_of(target * span, span), span)],
            dst_ref=regrouped.at[me],
            send_sem=send_sem.at[away],
            recv_sem=recv_sem.at[away],
            device_id={"tm": target},
            device_id_type=MESH,
        )

    @pl.loop(1, n)
    def _(away):
        piece(away).start()

    own = pltpu.make_async_copy(
        turned.at[pl.ds(pl.multiple_of(me * span, span), span)], regrouped.at[me], own_sem.at[0]
    )
    own.start()

    loads[1].wait()
    for level in range(table.shape[0]):
        other = table[level].T
        flipped[level] = other
        pairs[level] = right_pair(other)
    for chunk in range(count):
        prefix[chunk * STEPS] = flipped[levels[chunk * STEPS]]
    for step in range(1, STEPS):
        for chunk in range(count):
            t = chunk * STEPS + step
            prefix[t] = joined(
                jnp.dot(left_pair(prefix[t - 1]), pairs[levels[t]], preferred_element_type=F32)
            )
    spans = [prefix[chunk * STEPS + STEPS - 1] for chunk in range(count)]
    for chunk in range(count):
        ends[chunk] = spans[chunk].T if chunk % 2 else spans[chunk]
    width = 1
    while width < count:
        for chunk in range(count):
            if chunk & width:
                base = (chunk // width) * width - 1
                spans[chunk] = product(spans[base], spans[chunk])
        width *= 2
    total[0] = spans[count - 1]
    total[1] = spans[count - 1].T

    def shared(away):
        return pltpu.make_async_remote_copy(
            src_ref=total.at[lax.rem(place, 2)],
            dst_ref=maps.at[place],
            send_sem=msend_sem.at[away],
            recv_sem=mrecv_sem.at[away],
            device_id={"tm": home + lax.rem(place + away, group)},
            device_id_type=MESH,
        )

    for away in range(1, group):
        shared(away).start()
    kept = pltpu.make_async_copy(total.at[lax.rem(place, 2)], maps.at[place], own_sem.at[1])
    kept.start()
    for chunk in range(count - 1):
        heads[chunk] = spans[chunk].T

    for load in loads[2:]:
        load.wait()
    eye = diagonal(states)
    channels = lax.broadcasted_iota(jnp.int32, (states, pixels), 0)
    for k in range(n):
        projector[k] = jnp.where(
            modes[k : k + 1] == channels, weights[k : k + 1].astype(F32), 0.0
        ).astype(BF16)

    own.wait()

    @pl.loop(1, n)
    def _(away):
        piece(away).wait()

    measured = jnp.zeros((span, states), F32)
    for k in range(n):
        measured += lax.dot_general(
            regrouped[k], projector[k], (((1,), (1,)), ((), ())), preferred_element_type=F32
        )
    local[...] = lax.dot_general(
        measured.astype(BF16), gain[...], (((1,), (1,)), ((), ())), preferred_element_type=F32
    )
    held = [to_column(eye, local[c * STEPS : c * STEPS + 1]) for c in range(count)]
    for step in range(1, STEPS):
        for c in range(count):
            t = c * STEPS + step
            push = local[t : t + 1]
            if step % 2:
                held[c] = column_step(flipped[levels[t]], held[c], push)
                local[t : t + 1] = held[c]
            else:
                held[c] = row_step(eye, table[levels[t]], held[c], push)
                local[t : t + 1] = to_row(eye, held[c])
    carried = local[STEPS - 1 : STEPS]
    chunk_ends[0:1] = carried
    for c in range(1, count):
        push = local[c * STEPS + STEPS - 1 : c * STEPS + STEPS]
        if c % 2:
            carried = row_step(eye, ends[c], carried, push)
            chunk_ends[c : c + 1] = to_row(eye, carried)
        else:
            carried = column_step(ends[c], carried, push)
            chunk_ends[c : c + 1] = carried

    final = jnp.broadcast_to(chunk_ends[count - 1 : count], shift.shape)
    shift[...] = final
    shifts[place] = final

    def offsets(away):
        return pltpu.make_async_remote_copy(
            src_ref=shift,
            dst_ref=shifts.at[place],
            send_sem=csend_sem.at[away],
            recv_sem=crecv_sem.at[away],
            device_id={"tm": home + lax.rem(place + away, group)},
            device_id_type=MESH,
        )

    for away in range(1, group):
        offsets(away).start()
    kept.wait()
    for away in range(1, group):
        shared(away).wait()
    chain = maps[0].T
    for k in range(1, group):
        chain = product(maps[k] if k % 2 else maps[k].T, chain)
    whole[...] = chain
    for away in range(1, group):
        offsets(away).wait()

    moved = shifts[0, 0:1]
    for k in range(1, group):
        push = shifts[k, 0:1]
        moved = row_step(eye, maps[k], moved, push) if k % 2 else column_step(maps[k], moved, push)
    offset = moved if group % 2 else to_row(eye, moved)

    hop = pltpu.make_async_remote_copy(
        src_ref=leaving,
        dst_ref=arrived,
        send_sem=hop_send.at[0],
        recv_sem=hop_recv.at[0],
        device_id={"tm": lax.rem(me + group, n)},
        device_id_type=MESH,
    )

    @pl.when(has_last)
    def _():
        hop.wait_recv()

    @pl.when(jnp.logical_not(has_last))
    def _():
        arrived[...] = jnp.broadcast_to(start[...], arrived.shape)

    entry = arrived[0:1]

    @pl.when(has_next)
    def _():
        leaving[...] = jnp.broadcast_to(
            to_row(eye, row_step(eye, whole[...], entry, offset)), leaving.shape
        )
        hop.start()

    inside = entry
    column = to_column(eye, entry)
    for k in range(group - 1):
        push = shifts[k, 0:1]
        if k % 2:
            column = row_step(eye, maps[k], row, push)
            after = to_row(eye, column)
        else:
            row = column_step(maps[k], column, push)
            after = row
        inside = jnp.where(place == k + 1, after, inside)

    for c in range(count):
        if c:
            column = row_step(eye, heads[c - 1], inside, chunk_ends[c - 1 : c])
        else:
            column = to_column(eye, inside)
        for step in range(STEPS):
            t = c * STEPS + step
            out[t : t + 1] = column_step(prefix[t], column, local[t : t + 1])

    @pl.when(has_next)
    def _():
        hop.wait_send()


VMEM = pl.BlockSpec(memory_space=pltpu.VMEM)
SMEM = pl.BlockSpec(memory_space=pltpu.SMEM)
ANY = pl.BlockSpec(memory_space=pl.ANY)
LIMIT = 48 * 1024 * 1024


def shards(n, frames, levels, initial_state, transitions, gain, pixel_mode, pixel_weight):
    group = 4
    while n % group:
        group //= 2
    span = levels.shape[0]
    depth, states = transitions.shape[0], transitions.shape[1]
    pixels = frames.shape[0]
    count = span // STEPS
    square = (states, states)
    dma = pltpu.SemaphoreType.DMA
    return pl.pallas_call(
        functools.partial(fused_kernel, n, group),
        out_shape=jax.ShapeDtypeStruct((span, states), F32),
        in_specs=[SMEM] + [ANY] * 6,
        out_specs=VMEM,
        scratch_shapes=[
            pltpu.VMEM((pixels, n * span), BF16),
            pltpu.VMEM((n * span, pixels), BF16),
            pltpu.VMEM((n, span, pixels), BF16),
            pltpu.VMEM((depth, *square), F32),
            pltpu.VMEM((depth, *square), F32),
            pltpu.VMEM((depth, 2 * states, 2 * states), BF16),
            pltpu.VMEM((span, *square), F32),
            pltpu.VMEM((count, *square), F32),
            pltpu.VMEM((count, *square), F32),
            pltpu.VMEM((2, *square), F32),
            pltpu.VMEM((group, *square), F32),
            pltpu.VMEM(square, F32),
            pltpu.VMEM(square, BF16),
            pltpu.VMEM((n, pixels), jnp.int32),
            pltpu.VMEM((n, pixels), BF16),
            pltpu.VMEM((1, states), F32),
            pltpu.VMEM((n, states, pixels), BF16),
            pltpu.VMEM((span, states), F32),
            pltpu.VMEM((count, states), F32),
            pltpu.VMEM((8, states), F32),
            pltpu.VMEM((group, 8, states), F32),
            pltpu.VMEM((8, states), F32),
            pltpu.VMEM((8, states), F32),
            dma((6,)),
            dma((2,)),
            dma((n,)),
            dma((n,)),
            dma((group,)),
            dma((group,)),
            dma((group,)),
            dma((group,)),
            dma((1,)),
            dma((1,)),
        ],
        compiler_params=pltpu.CompilerParams(
            collective_id=0, has_side_effects=True, vmem_limit_bytes=LIMIT
        ),
        name="filter",
    )(
        levels,
        frames,
        transitions,
        gain,
        pixel_mode.reshape(n, pixels),
        pixel_weight.reshape(n, pixels),
        initial_state.reshape(1, states),
    )


def solution(mesh):
    in_specs = (P("tm", "parts"), P(("parts", "tm")), P("parts"), P(), P(), P(), P())
    out_specs = P(("parts", "tm"), None)
    return jax.shard_map(
        functools.partial(shards, mesh.shape["tm"]),
        mesh=mesh,
        in_specs=in_specs,
        out_specs=out_specs,
        check_vma=False,
    )
```

```python
import functools

import jax
import jax.numpy as jnp
from jax import lax
from jax.experimental import pallas as pl
from jax.experimental.pallas import tpu as pltpu
from jax.sharding import PartitionSpec as P

MESH = pl.DeviceIdType.MESH
F32 = jnp.float32
BF16 = jnp.bfloat16
STEPS = 8


def halves(x):
    high = x.astype(BF16)
    return high, (x - high.astype(F32)).astype(BF16)


def left_pair(x):
    high, low = halves(x)
    return jnp.concatenate([high, low], axis=1)


def right_pair(y):
    pair = left_pair(y)
    return jnp.concatenate([pair, pair], axis=0)


def joined(pair):
    return pair[:, : pair.shape[1] // 2] + pair[:, pair.shape[1] // 2 :]


def product(x, y):
    return joined(jnp.dot(left_pair(x), right_pair(y), preferred_element_type=F32))


def diagonal(size):
    return lax.broadcasted_iota(jnp.int32, (size, size), 0) == lax.broadcasted_iota(
        jnp.int32, (size, size), 1
    )


def to_column(eye, row):
    return jnp.sum(jnp.where(eye, row, 0.0), axis=1, keepdims=True)


def to_row(eye, column):
    return jnp.sum(jnp.where(eye, column, 0.0), axis=0, keepdims=True)


def row_step(eye, matrix, row, push):
    return jnp.sum(matrix * row + jnp.where(eye, push, 0.0), axis=1, keepdims=True)


def column_step(flipped, column, push):
    return jnp.sum(flipped * column, axis=0, keepdims=True) + push


def fused_kernel(
    n, group,
    levels, frames_in, table_in, gain_in, modes_in, weights_in, start_in,
    out,
    raw, turned, regrouped, table, flipped, pairs, prefix, heads, ends, total, maps, whole,
    gain, modes, weights, start, projector, local, chunk_ends, shift, shifts, block_maps, block_shifts, message, entering,
    load_sem, own_sem, send_sem, recv_sem, msend_sem, mrecv_sem, csend_sem, crecv_sem, wsend_sem, wrecv_sem, hsend_sem, hrecv_sem,
):
    me = lax.axis_index("tm")
    place = lax.rem(me, group)
    home = me - place
    block, blocks = me // group, n // group
    span = out.shape[0]
    states = gain.shape[0]
    pixels = raw.shape[0]
    count = span // STEPS
    loads = [
        pltpu.make_async_copy(source, target, load_sem.at[i])
        for i, (source, target) in enumerate(
            [(frames_in, raw), (table_in, table), (gain_in, gain), (modes_in, modes), (weights_in, weights), (start_in, start)]
        )
    ]
    for load in loads:
        load.start()
    barrier = pltpu.get_barrier_semaphore()

    @pl.loop(1, n)
    def _(away):
        pl.semaphore_signal(barrier, inc=1, device_id={"tm": lax.rem(me + away, n)}, device_id_type=MESH)

    loads[0].wait()
    for at in range(0, n * span, 128):
        turned[at : at + 128] = raw[:, at : at + 128].T
    pl.semaphore_wait(barrier, n - 1)

    def piece(away):
        target = lax.rem(me + away, n)
        return pltpu.make_async_remote_copy(
            src_ref=turned.at[pl.ds(pl.multiple_of(target * span, span), span)],
            dst_ref=regrouped.at[me],
            send_sem=send_sem.at[away],
            recv_sem=recv_sem.at[away],
            device_id={"tm": target},
            device_id_type=MESH,
        )

    @pl.loop(1, n)
    def _(away):
        piece(away).start()

    own = pltpu.make_async_copy(
        turned.at[pl.ds(pl.multiple_of(me * span, span), span)], regrouped.at[me], own_sem.at[0]
    )
    own.start()

    loads[1].wait()
    for level in range(table.shape[0]):
        other = table[level].T
        flipped[level] = other
        pairs[level] = right_pair(other)
    for chunk in range(count):
        prefix[chunk * STEPS] = flipped[levels[chunk * STEPS]]
    for step in range(1, STEPS):
        for chunk in range(count):
            t = chunk * STEPS + step
            prefix[t] = joined(
                jnp.dot(left_pair(prefix[t - 1]), pairs[levels[t]], preferred_element_type=F32)
            )
    spans = [prefix[chunk * STEPS + STEPS - 1] for chunk in range(count)]
    for chunk in range(count):
        ends[chunk] = spans[chunk].T if chunk % 2 else spans[chunk]
    width = 1
    while width < count:
        for chunk in range(count):
            if chunk & width:
                base = (chunk // width) * width - 1
                spans[chunk] = product(spans[base], spans[chunk])
        width *= 2
    total[0] = spans[count - 1]
    total[1] = spans[count - 1].T

    def shared(away):
        return pltpu.make_async_remote_copy(
            src_ref=total.at[lax.rem(place, 2)],
            dst_ref=maps.at[place],
            send_sem=msend_sem.at[away],
            recv_sem=mrecv_sem.at[away],
            device_id={"tm": home + lax.rem(place + away, group)},
            device_id_type=MESH,
        )

    for away in range(1, group):
        shared(away).start()
    kept = pltpu.make_async_copy(total.at[lax.rem(place, 2)], maps.at[place], own_sem.at[1])
    kept.start()
    for chunk in range(count - 1):
        heads[chunk] = spans[chunk].T

    for load in loads[2:]:
        load.wait()
    eye = diagonal(states)
    channels = lax.broadcasted_iota(jnp.int32, (states, pixels), 0)
    for k in range(n):
        projector[k] = jnp.where(
            modes[k : k + 1] == channels, weights[k : k + 1].astype(F32), 0.0
        ).astype(BF16)

    kept.wait()
    for away in range(1, group):
        shared(away).wait()
    chain = maps[0].T
    for k in range(1, group):
        chain = product(maps[k] if k % 2 else maps[k].T, chain)
    whole[...] = chain

    def forward(hops):
        return pltpu.make_async_remote_copy(
            src_ref=whole,
            dst_ref=block_maps.at[block],
            send_sem=wsend_sem.at[hops],
            recv_sem=wrecv_sem.at[hops],
            device_id={"tm": lax.rem(me + hops * group, n)},
            device_id_type=MESH,
        )

    for hops in range(1, blocks):

        @pl.when(jnp.logical_and(block > 0, block + hops < blocks))
        def _():
            forward(hops).start()

    seeded = jnp.where(block == 0, to_row(eye, row_step(eye, chain, start[...], 0.0)), 0.0)
    own.wait()

    @pl.loop(1, n)
    def _(away):
        piece(away).wait()

    measured = jnp.zeros((span, states), F32)
    for k in range(n):
        measured += lax.dot_general(
            regrouped[k], projector[k], (((1,), (1,)), ((), ())), preferred_element_type=F32
        )
    local[...] = lax.dot_general(
        measured.astype(BF16), gain[...], (((1,), (1,)), ((), ())), preferred_element_type=F32
    )
    held = [to_column(eye, local[c * STEPS : c * STEPS + 1]) for c in range(count)]
    for step in range(1, STEPS):
        for c in range(count):
            t = c * STEPS + step
            push = local[t : t + 1]
            if step % 2:
                held[c] = column_step(flipped[levels[t]], held[c], push)
                local[t : t + 1] = held[c]
            else:
                held[c] = row_step(eye, table[levels[t]], held[c], push)
                local[t : t + 1] = to_row(eye, held[c])
    carried = local[STEPS - 1 : STEPS]
    chunk_ends[0:1] = carried
    for c in range(1, count):
        push = local[c * STEPS + STEPS - 1 : c * STEPS + STEPS]
        if c % 2:
            carried = row_step(eye, ends[c], carried, push)
            chunk_ends[c : c + 1] = to_row(eye, carried)
        else:
            carried = column_step(ends[c], carried, push)
            chunk_ends[c : c + 1] = carried

    final = jnp.broadcast_to(chunk_ends[count - 1 : count], shift.shape)
    shift[...] = final
    shifts[place] = final

    def offsets(away):
        return pltpu.make_async_remote_copy(
            src_ref=shift,
            dst_ref=shifts.at[place],
            send_sem=csend_sem.at[away],
            recv_sem=crecv_sem.at[away],
            device_id={"tm": home + lax.rem(place + away, group)},
            device_id_type=MESH,
        )

    for away in range(1, group):
        offsets(away).start()
    for away in range(1, group):
        offsets(away).wait()

    moved = shifts[0, 0:1]
    for k in range(1, group):
        push = shifts[k, 0:1]
        moved = row_step(eye, maps[k], moved, push) if k % 2 else column_step(maps[k], moved, push)
    offset = moved if group % 2 else to_row(eye, moved)

    message[...] = jnp.broadcast_to(offset + seeded, message.shape)

    def ahead(hops):
        return pltpu.make_async_remote_copy(
            src_ref=message,
            dst_ref=block_shifts.at[block],
            send_sem=hsend_sem.at[hops],
            recv_sem=hrecv_sem.at[hops],
            device_id={"tm": lax.rem(me + hops * group, n)},
            device_id_type=MESH,
        )

    for hops in range(1, blocks):

        @pl.when(block + hops < blocks)
        def _():
            ahead(hops).start()

    for hops in range(1, blocks):

        @pl.when(block > hops)
        def _():
            forward(hops).wait_recv()

        @pl.when(block >= hops)
        def _():
            ahead(hops).wait_recv()

    entering[...] = start[...]

    @pl.when(block > 0)
    def _():
        entering[...] = block_shifts[0, 0:1]

    for k in range(1, blocks - 1):

        @pl.when(block > k)
        def _():
            entering[...] = to_row(
                eye, row_step(eye, block_maps[k], entering[...], block_shifts[k, 0:1])
            )

    entry = entering[...]
    inside = entry
    column = to_column(eye, entry)
    for k in range(group - 1):
        push = shifts[k, 0:1]
        if k % 2:
            column = row_step(eye, maps[k], row, push)
            after = to_row(eye, column)
        else:
            row = column_step(maps[k], column, push)
            after = row
        inside = jnp.where(place == k + 1, after, inside)

    for c in range(count):
        if c:
            column = row_step(eye, heads[c - 1], inside, chunk_ends[c - 1 : c])
        else:
            column = to_column(eye, inside)
        for step in range(STEPS):
            t = c * STEPS + step
            out[t : t + 1] = column_step(prefix[t], column, local[t : t + 1])

    for hops in range(1, blocks):

        @pl.when(jnp.logical_and(block > 0, block + hops < blocks))
        def _():
            forward(hops).wait_send()

        @pl.when(block + hops < blocks)
        def _():
            ahead(hops).wait_send()


VMEM = pl.BlockSpec(memory_space=pltpu.VMEM)
SMEM = pl.BlockSpec(memory_space=pltpu.SMEM)
HBM = pl.BlockSpec(memory_space=pltpu.HBM)
LIMIT = 63 * 1024 * 1024


def shards(n, frames, levels, initial_state, transitions, gain, pixel_mode, pixel_weight):
    group = 4
    while n % group:
        group //= 2
    span = levels.shape[0]
    depth, states = transitions.shape[0], transitions.shape[1]
    pixels = frames.shape[0]
    count = span // STEPS
    square = (states, states)
    dma = pltpu.SemaphoreType.DMA
    return pl.pallas_call(
        functools.partial(fused_kernel, n, group),
        out_shape=jax.ShapeDtypeStruct((span, states), F32),
        in_specs=[SMEM] + [HBM] * 6,
        out_specs=VMEM,
        scratch_shapes=[
            pltpu.VMEM((pixels, n * span), BF16),
            pltpu.VMEM((n * span, pixels), BF16),
            pltpu.VMEM((n, span, pixels), BF16),
            pltpu.VMEM((depth, *square), F32),
            pltpu.VMEM((depth, *square), F32),
            pltpu.VMEM((depth, 2 * states, 2 * states), BF16),
            pltpu.VMEM((span, *square), F32),
            pltpu.VMEM((count, *square), F32),
            pltpu.VMEM((count, *square), F32),
            pltpu.VMEM((2, *square), F32),
            pltpu.VMEM((group, *square), F32),
            pltpu.VMEM(square, F32),
            pltpu.VMEM(square, BF16),
            pltpu.VMEM((n, pixels), jnp.int32),
            pltpu.VMEM((n, pixels), BF16),
            pltpu.VMEM((1, states), F32),
            pltpu.VMEM((n, states, pixels), BF16),
            pltpu.VMEM((span, states), F32),
            pltpu.VMEM((count, states), F32),
            pltpu.VMEM((8, states), F32),
            pltpu.VMEM((group, 8, states), F32),
            pltpu.VMEM((n // group, *square), F32),
            pltpu.VMEM((n // group, 8, states), F32),
            pltpu.VMEM((8, states), F32),
            pltpu.VMEM((1, states), F32),
            dma((6,)),
            dma((2,)),
            dma((n,)),
            dma((n,)),
            dma((group,)),
            dma((group,)),
            dma((group,)),
            dma((group,)),
            dma((n // group,)),
            dma((n // group,)),
            dma((n // group,)),
            dma((n // group,)),
        ],
        compiler_params=pltpu.CompilerParams(
            collective_id=0, has_side_effects=True, vmem_limit_bytes=LIMIT
        ),
        name="filter",
    )(
        levels,
        frames,
        transitions,
        gain,
        pixel_mode.reshape(n, pixels),
        pixel_weight.reshape(n, pixels),
        initial_state.reshape(1, states),
    )


def solution(mesh):
    in_specs = (P("tm", "parts"), P(("parts", "tm")), P("parts"), P(), P(), P(), P())
    out_specs = P(("parts", "tm"), None)
    return jax.shard_map(
        functools.partial(shards, mesh.shape["tm"]),
        mesh=mesh,
        in_specs=in_specs,
        out_specs=out_specs,
        check_vma=False,
    )
```

```python
import functools

import jax
import jax.numpy as jnp
from jax import lax
from jax.experimental import pallas as pl
from jax.experimental.pallas import tpu as pltpu
from jax.sharding import PartitionSpec as P

MESH = pl.DeviceIdType.MESH
F32 = jnp.float32
BF16 = jnp.bfloat16
STEPS = 8


def halves(x):
    high = x.astype(BF16)
    return high, (x - high.astype(F32)).astype(BF16)


def left_pair(x):
    high, low = halves(x)
    return jnp.concatenate([high, low], axis=1)


def right_pair(y):
    pair = left_pair(y)
    return jnp.concatenate([pair, pair], axis=0)


def joined(pair):
    return pair[:, : pair.shape[1] // 2] + pair[:, pair.shape[1] // 2 :]


def product(x, y):
    return joined(jnp.dot(left_pair(x), right_pair(y), preferred_element_type=F32))


def diagonal(size):
    return lax.broadcasted_iota(jnp.int32, (size, size), 0) == lax.broadcasted_iota(
        jnp.int32, (size, size), 1
    )


def to_column(eye, row):
    return jnp.sum(jnp.where(eye, row, 0.0), axis=1, keepdims=True)


def to_row(eye, column):
    return jnp.sum(jnp.where(eye, column, 0.0), axis=0, keepdims=True)


def row_step(eye, matrix, row, push):
    return jnp.sum(matrix * row + jnp.where(eye, push, 0.0), axis=1, keepdims=True)


def column_step(flipped, column, push):
    return jnp.sum(flipped * column, axis=0, keepdims=True) + push


def fused_kernel(
    n, group,
    levels, frames_in, table_in, gain_in, modes_in, weights_in, start_in,
    out,
    raw, turned, regrouped, table, flipped, pairs, prefix, heads, ends, total, maps, whole,
    gain, modes, weights, start, projector, local, chunk_ends, shift, shifts, block_maps, block_shifts, message, entering,
    load_sem, own_sem, send_sem, recv_sem, msend_sem, mrecv_sem, csend_sem, crecv_sem, wsend_sem, wrecv_sem, hsend_sem, hrecv_sem,
):
    me = lax.axis_index("tm")
    place = lax.rem(me, group)
    home = me - place
    block, blocks = me // group, n // group
    span = out.shape[0]
    states = gain.shape[0]
    pixels = raw.shape[0]
    count = span // STEPS
    loads = [
        pltpu.make_async_copy(source, target, load_sem.at[i])
        for i, (source, target) in enumerate(
            [(frames_in, raw), (table_in, table), (gain_in, gain), (modes_in, modes), (weights_in, weights), (start_in, start)]
        )
    ]
    for load in loads:
        load.start()
    barrier = pltpu.get_barrier_semaphore()

    @pl.loop(1, n)
    def _(away):
        pl.semaphore_signal(barrier, inc=1, device_id={"tm": lax.rem(me + away, n)}, device_id_type=MESH)

    loads[0].wait()
    for at in range(0, n * span, 128):
        turned[at : at + 128] = raw[:, at : at + 128].T
    loads[1].wait()
    for level in range(table.shape[0]):
        other = table[level].T
        flipped[level] = other
        pairs[level] = right_pair(other)
    pl.semaphore_wait(barrier, n - 1)

    def piece(away):
        target = lax.rem(me + away, n)
        return pltpu.make_async_remote_copy(
            src_ref=turned.at[pl.ds(pl.multiple_of(target * span, span), span)],
            dst_ref=regrouped.at[me],
            send_sem=send_sem.at[away],
            recv_sem=recv_sem.at[away],
            device_id={"tm": target},
            device_id_type=MESH,
        )

    @pl.loop(0, n - 1)
    def _(turn):
        piece(n // 2 + (1 - 2 * lax.rem(turn, 2)) * ((turn + 1) // 2)).start()

    own = pltpu.make_async_copy(
        turned.at[pl.ds(pl.multiple_of(me * span, span), span)], regrouped.at[me], own_sem.at[0]
    )
    own.start()

    for chunk in range(count):
        prefix[chunk * STEPS] = flipped[levels[chunk * STEPS]]
    for step in range(1, STEPS):
        for chunk in range(count):
            t = chunk * STEPS + step
            prefix[t] = joined(
                jnp.dot(left_pair(prefix[t - 1]), pairs[levels[t]], preferred_element_type=F32)
            )
    spans = [prefix[chunk * STEPS + STEPS - 1] for chunk in range(count)]
    for chunk in range(count):
        ends[chunk] = spans[chunk].T if chunk % 2 else spans[chunk]
    width = 1
    while width < count:
        for chunk in range(count):
            if chunk & width:
                base = (chunk // width) * width - 1
                spans[chunk] = product(spans[base], spans[chunk])
        width *= 2
    total[0] = spans[count - 1]
    total[1] = spans[count - 1].T

    def shared(away):
        return pltpu.make_async_remote_copy(
            src_ref=total.at[lax.rem(place, 2)],
            dst_ref=maps.at[place],
            send_sem=msend_sem.at[away],
            recv_sem=mrecv_sem.at[away],
            device_id={"tm": home + lax.rem(place + away, group)},
            device_id_type=MESH,
        )

    for away in range(1, group):
        shared(away).start()
    kept = pltpu.make_async_copy(total.at[lax.rem(place, 2)], maps.at[place], own_sem.at[1])
    kept.start()
    for chunk in range(count - 1):
        heads[chunk] = spans[chunk].T

    for load in loads[2:]:
        load.wait()
    eye = diagonal(states)
    channels = lax.broadcasted_iota(jnp.int32, (states, pixels), 0)
    for k in range(n):
        projector[k] = jnp.where(
            modes[k : k + 1] == channels, weights[k : k + 1].astype(F32), 0.0
        ).astype(BF16)

    own.wait()

    @pl.loop(1, n)
    def _(away):
        piece(away).wait()

    measured = jnp.zeros((span, states), F32)
    for k in range(n):
        measured += lax.dot_general(
            regrouped[k], projector[k], (((1,), (1,)), ((), ())), preferred_element_type=F32
        )
    local[...] = lax.dot_general(
        measured.astype(BF16), gain[...], (((1,), (1,)), ((), ())), preferred_element_type=F32
    )
    held = [to_column(eye, local[c * STEPS : c * STEPS + 1]) for c in range(count)]
    for step in range(1, STEPS):
        for c in range(count):
            t = c * STEPS + step
            push = local[t : t + 1]
            if step % 2:
                held[c] = column_step(flipped[levels[t]], held[c], push)
                local[t : t + 1] = held[c]
            else:
                held[c] = row_step(eye, table[levels[t]], held[c], push)
                local[t : t + 1] = to_row(eye, held[c])
    carried = local[STEPS - 1 : STEPS]
    chunk_ends[0:1] = carried
    for c in range(1, count):
        push = local[c * STEPS + STEPS - 1 : c * STEPS + STEPS]
        if c % 2:
            carried = row_step(eye, ends[c], carried, push)
            chunk_ends[c : c + 1] = to_row(eye, carried)
        else:
            carried = column_step(ends[c], carried, push)
            chunk_ends[c : c + 1] = carried

    final = jnp.broadcast_to(chunk_ends[count - 1 : count], shift.shape)
    shift[...] = final
    shifts[place] = final

    def offsets(away):
        return pltpu.make_async_remote_copy(
            src_ref=shift,
            dst_ref=shifts.at[place],
            send_sem=csend_sem.at[away],
            recv_sem=crecv_sem.at[away],
            device_id={"tm": home + lax.rem(place + away, group)},
            device_id_type=MESH,
        )

    for away in range(1, group):
        offsets(away).start()
    kept.wait()
    for away in range(1, group):
        shared(away).wait()
    chain = maps[0].T
    for k in range(1, group):
        chain = product(maps[k] if k % 2 else maps[k].T, chain)
    whole[...] = chain

    def forward(hops):
        return pltpu.make_async_remote_copy(
            src_ref=whole,
            dst_ref=block_maps.at[block],
            send_sem=wsend_sem.at[hops],
            recv_sem=wrecv_sem.at[hops],
            device_id={"tm": lax.rem(me + hops * group, n)},
            device_id_type=MESH,
        )

    for hops in range(1, blocks):

        @pl.when(jnp.logical_and(block > 0, block + hops < blocks))
        def _():
            forward(hops).start()

    seeded = jnp.where(block == 0, to_row(eye, row_step(eye, chain, start[...], 0.0)), 0.0)
    for away in range(1, group):
        offsets(away).wait()

    moved = shifts[0, 0:1]
    for k in range(1, group):
        push = shifts[k, 0:1]
        moved = row_step(eye, maps[k], moved, push) if k % 2 else column_step(maps[k], moved, push)
    offset = moved if group % 2 else to_row(eye, moved)

    message[...] = jnp.broadcast_to(offset + seeded, message.shape)

    def ahead(hops):
        return pltpu.make_async_remote_copy(
            src_ref=message,
            dst_ref=block_shifts.at[block],
            send_sem=hsend_sem.at[hops],
            recv_sem=hrecv_sem.at[hops],
            device_id={"tm": lax.rem(me + hops * group, n)},
            device_id_type=MESH,
        )

    for hops in range(1, blocks):

        @pl.when(block + hops < blocks)
        def _():
            ahead(hops).start()

    for hops in range(1, blocks):

        @pl.when(block > hops)
        def _():
            forward(hops).wait_recv()

        @pl.when(block >= hops)
        def _():
            ahead(hops).wait_recv()

    entering[...] = start[...]

    @pl.when(block > 0)
    def _():
        entering[...] = block_shifts[0, 0:1]

    for k in range(1, blocks - 1):

        @pl.when(block > k)
        def _():
            entering[...] = to_row(
                eye, row_step(eye, block_maps[k], entering[...], block_shifts[k, 0:1])
            )

    entry = entering[...]
    inside = entry
    column = to_column(eye, entry)
    for k in range(group - 1):
        push = shifts[k, 0:1]
        if k % 2:
            column = row_step(eye, maps[k], row, push)
            after = to_row(eye, column)
        else:
            row = column_step(maps[k], column, push)
            after = row
        inside = jnp.where(place == k + 1, after, inside)

    for c in range(count):
        if c:
            column = row_step(eye, heads[c - 1], inside, chunk_ends[c - 1 : c])
        else:
            column = to_column(eye, inside)
        for step in range(STEPS):
            t = c * STEPS + step
            out[t : t + 1] = column_step(prefix[t], column, local[t : t + 1])

    for hops in range(1, blocks):

        @pl.when(jnp.logical_and(block > 0, block + hops < blocks))
        def _():
            forward(hops).wait_send()

        @pl.when(block + hops < blocks)
        def _():
            ahead(hops).wait_send()


VMEM = pl.BlockSpec(memory_space=pltpu.VMEM)
SMEM = pl.BlockSpec(memory_space=pltpu.SMEM)
HBM = pl.BlockSpec(memory_space=pltpu.HBM)
LIMIT = 63 * 1024 * 1024


def shards(n, frames, levels, initial_state, transitions, gain, pixel_mode, pixel_weight):
    group = 4
    while n % group:
        group //= 2
    span = levels.shape[0]
    depth, states = transitions.shape[0], transitions.shape[1]
    pixels = frames.shape[0]
    count = span // STEPS
    square = (states, states)
    dma = pltpu.SemaphoreType.DMA
    return pl.pallas_call(
        functools.partial(fused_kernel, n, group),
        out_shape=jax.ShapeDtypeStruct((span, states), F32),
        in_specs=[SMEM] + [HBM] * 6,
        out_specs=VMEM,
        scratch_shapes=[
            pltpu.VMEM((pixels, n * span), BF16),
            pltpu.VMEM((n * span, pixels), BF16),
            pltpu.VMEM((n, span, pixels), BF16),
            pltpu.VMEM((depth, *square), F32),
            pltpu.VMEM((depth, *square), F32),
            pltpu.VMEM((depth, 2 * states, 2 * states), BF16),
            pltpu.VMEM((span, *square), F32),
            pltpu.VMEM((count, *square), F32),
            pltpu.VMEM((count, *square), F32),
            pltpu.VMEM((2, *square), F32),
            pltpu.VMEM((group, *square), F32),
            pltpu.VMEM(square, F32),
            pltpu.VMEM(square, BF16),
            pltpu.VMEM((n, pixels), jnp.int32),
            pltpu.VMEM((n, pixels), BF16),
            pltpu.VMEM((1, states), F32),
            pltpu.VMEM((n, states, pixels), BF16),
            pltpu.VMEM((span, states), F32),
            pltpu.VMEM((count, states), F32),
            pltpu.VMEM((8, states), F32),
            pltpu.VMEM((group, 8, states), F32),
            pltpu.VMEM((n // group, *square), F32),
            pltpu.VMEM((n // group, 8, states), F32),
            pltpu.VMEM((8, states), F32),
            pltpu.VMEM((1, states), F32),
            dma((6,)),
            dma((2,)),
            dma((n,)),
            dma((n,)),
            dma((group,)),
            dma((group,)),
            dma((group,)),
            dma((group,)),
            dma((n // group,)),
            dma((n // group,)),
            dma((n // group,)),
            dma((n // group,)),
        ],
        compiler_params=pltpu.CompilerParams(
            collective_id=0, has_side_effects=True, vmem_limit_bytes=LIMIT
        ),
        name="filter",
    )(
        levels,
        frames,
        transitions,
        gain,
        pixel_mode.reshape(n, pixels),
        pixel_weight.reshape(n, pixels),
        initial_state.reshape(1, states),
    )


def solution(mesh):
    in_specs = (P("tm", "parts"), P(("parts", "tm")), P("parts"), P(), P(), P(), P())
    out_specs = P(("parts", "tm"), None)
    return jax.shard_map(
        functools.partial(shards, mesh.shape["tm"]),
        mesh=mesh,
        in_specs=in_specs,
        out_specs=out_specs,
        check_vma=False,
    )
```

```python
import functools

import jax
import jax.numpy as jnp
from jax import lax
from jax.experimental import pallas as pl
from jax.experimental.pallas import tpu as pltpu
from jax.sharding import PartitionSpec as P

MESH = pl.DeviceIdType.MESH
F32 = jnp.float32
BF16 = jnp.bfloat16
STEPS = 8


def halves(x):
    high = x.astype(BF16)
    return high, (x - high.astype(F32)).astype(BF16)


def left_pair(x):
    high, low = halves(x)
    return jnp.concatenate([high, low], axis=1)


def right_pair(y):
    pair = left_pair(y)
    return jnp.concatenate([pair, pair], axis=0)


def joined(pair):
    return pair[:, : pair.shape[1] // 2] + pair[:, pair.shape[1] // 2 :]


def product(x, y):
    return joined(jnp.dot(left_pair(x), right_pair(y), preferred_element_type=F32))


def diagonal(size):
    return lax.broadcasted_iota(jnp.int32, (size, size), 0) == lax.broadcasted_iota(
        jnp.int32, (size, size), 1
    )


def to_column(eye, row):
    return jnp.sum(jnp.where(eye, row, 0.0), axis=1, keepdims=True)


def to_row(eye, column):
    return jnp.sum(jnp.where(eye, column, 0.0), axis=0, keepdims=True)


def row_step(eye, matrix, row, push):
    return jnp.sum(matrix * row + jnp.where(eye, push, 0.0), axis=1, keepdims=True)


def column_step(flipped, column, push):
    return jnp.sum(flipped * column, axis=0, keepdims=True) + push


def fused_kernel(
    n, group,
    levels, frames_in, table_in, gain_in, modes_in, weights_in, start_in,
    out,
    raw, turned, regrouped, table, flipped, pairs, prefix, heads, ends, total, maps, whole,
    gain, modes, weights, start, projector, local, chunk_ends, shift, shifts, block_maps, block_shifts, message, entering,
    load_sem, own_sem, send_sem, recv_sem, msend_sem, mrecv_sem, csend_sem, crecv_sem, wsend_sem, wrecv_sem, hsend_sem, hrecv_sem,
):
    me = lax.axis_index("tm")
    place = lax.rem(me, group)
    home = me - place
    block, blocks = me // group, n // group
    span = out.shape[0]
    states = gain.shape[0]
    pixels = raw.shape[0]
    count = span // STEPS
    loads = [
        pltpu.make_async_copy(source, target, load_sem.at[i])
        for i, (source, target) in enumerate(
            [(frames_in, raw), (table_in, table), (gain_in, gain), (modes_in, modes), (weights_in, weights), (start_in, start)]
        )
    ]
    for load in loads:
        load.start()
    barrier = pltpu.get_barrier_semaphore()

    @pl.loop(1, n)
    def _(away):
        pl.semaphore_signal(barrier, inc=1, device_id={"tm": lax.rem(me + away, n)}, device_id_type=MESH)

    loads[0].wait()
    for at in range(0, n * span, 128):
        turned[at : at + 128] = raw[:, at : at + 128].T
    loads[1].wait()
    for level in range(table.shape[0]):
        other = table[level].T
        flipped[level] = other
        pairs[level] = right_pair(other)
    pl.semaphore_wait(barrier, n - 1)

    def piece(away):
        target = lax.rem(me + away, n)
        return pltpu.make_async_remote_copy(
            src_ref=turned.at[pl.ds(pl.multiple_of(target * span, span), span)],
            dst_ref=regrouped.at[me],
            send_sem=send_sem.at[away],
            recv_sem=recv_sem.at[away],
            device_id={"tm": target},
            device_id_type=MESH,
        )

    @pl.loop(0, n - 1)
    def _(turn):
        piece(n // 2 + (1 - 2 * lax.rem(turn, 2)) * ((turn + 1) // 2)).start()

    own = pltpu.make_async_copy(
        turned.at[pl.ds(pl.multiple_of(me * span, span), span)], regrouped.at[me], own_sem.at[0]
    )
    own.start()

    for chunk in range(count):
        prefix[chunk * STEPS] = flipped[levels[chunk * STEPS]]
    for step in range(1, STEPS):
        for chunk in range(count):
            t = chunk * STEPS + step
            prefix[t] = joined(
                jnp.dot(left_pair(prefix[t - 1]), pairs[levels[t]], preferred_element_type=F32)
            )
    spans = [prefix[chunk * STEPS + STEPS - 1] for chunk in range(count)]
    tree = [spans]
    while len(tree[-1]) > 1:
        last = tree[-1]
        tree.append([product(last[2 * k], last[2 * k + 1]) for k in range(len(last) // 2)])
    total[0] = tree[-1][0]
    total[1] = tree[-1][0].T

    def shared(away):
        return pltpu.make_async_remote_copy(
            src_ref=total.at[lax.rem(place, 2)],
            dst_ref=maps.at[place],
            send_sem=msend_sem.at[away],
            recv_sem=mrecv_sem.at[away],
            device_id={"tm": home + lax.rem(place + away, group)},
            device_id_type=MESH,
        )

    for away in range(1, group):
        shared(away).start()
    kept = pltpu.make_async_copy(total.at[lax.rem(place, 2)], maps.at[place], own_sem.at[1])
    kept.start()
    for chunk in range(count):
        ends[chunk] = spans[chunk].T if chunk % 2 else spans[chunk]
    reached = [None]
    for upto in range(1, count):
        rank = (upto & -upto).bit_length() - 1
        node = tree[rank][(upto >> rank) - 1]
        before = reached[upto - (1 << rank)]
        reached.append(node if before is None else product(before, node))
        heads[upto - 1] = reached[upto].T

    for load in loads[2:]:
        load.wait()
    eye = diagonal(states)
    channels = lax.broadcasted_iota(jnp.int32, (states, pixels), 0)
    for k in range(n):
        projector[k] = jnp.where(
            modes[k : k + 1] == channels, weights[k : k + 1].astype(F32), 0.0
        ).astype(BF16)

    own.wait()

    @pl.loop(1, n)
    def _(away):
        piece(away).wait()

    measured = jnp.zeros((span, states), F32)
    for k in range(n):
        measured += lax.dot_general(
            regrouped[k], projector[k], (((1,), (1,)), ((), ())), preferred_element_type=F32
        )
    local[...] = lax.dot_general(
        measured.astype(BF16), gain[...], (((1,), (1,)), ((), ())), preferred_element_type=F32
    )
    held = [to_column(eye, local[c * STEPS : c * STEPS + 1]) for c in range(count)]
    for step in range(1, STEPS):
        for c in range(count):
            t = c * STEPS + step
            push = local[t : t + 1]
            if step % 2:
                held[c] = column_step(flipped[levels[t]], held[c], push)
                local[t : t + 1] = held[c]
            else:
                held[c] = row_step(eye, table[levels[t]], held[c], push)
                local[t : t + 1] = to_row(eye, held[c])
    carried = local[STEPS - 1 : STEPS]
    chunk_ends[0:1] = carried
    for c in range(1, count):
        push = local[c * STEPS + STEPS - 1 : c * STEPS + STEPS]
        if c % 2:
            carried = row_step(eye, ends[c], carried, push)
            chunk_ends[c : c + 1] = to_row(eye, carried)
        else:
            carried = column_step(ends[c], carried, push)
            chunk_ends[c : c + 1] = carried

    final = jnp.broadcast_to(chunk_ends[count - 1 : count], shift.shape)
    shift[...] = final
    shifts[place] = final

    def offsets(away):
        return pltpu.make_async_remote_copy(
            src_ref=shift,
            dst_ref=shifts.at[place],
            send_sem=csend_sem.at[away],
            recv_sem=crecv_sem.at[away],
            device_id={"tm": home + lax.rem(place + away, group)},
            device_id_type=MESH,
        )

    for away in range(1, group):
        offsets(away).start()
    kept.wait()
    for away in range(1, group):
        shared(away).wait()
    chain = maps[0].T
    for k in range(1, group):
        chain = product(maps[k] if k % 2 else maps[k].T, chain)
    whole[...] = chain

    def forward(hops):
        return pltpu.make_async_remote_copy(
            src_ref=whole,
            dst_ref=block_maps.at[block],
            send_sem=wsend_sem.at[hops],
            recv_sem=wrecv_sem.at[hops],
            device_id={"tm": lax.rem(me + hops * group, n)},
            device_id_type=MESH,
        )

    for hops in range(1, blocks):

        @pl.when(jnp.logical_and(block > 0, block + hops < blocks))
        def _():
            forward(hops).start()

    seeded = jnp.where(block == 0, to_row(eye, row_step(eye, chain, start[...], 0.0)), 0.0)
    for away in range(1, group):
        offsets(away).wait()

    moved = shifts[0, 0:1]
    for k in range(1, group):
        push = shifts[k, 0:1]
        moved = row_step(eye, maps[k], moved, push) if k % 2 else column_step(maps[k], moved, push)
    offset = moved if group % 2 else to_row(eye, moved)

    message[...] = jnp.broadcast_to(offset + seeded, message.shape)

    def ahead(hops):
        return pltpu.make_async_remote_copy(
            src_ref=message,
            dst_ref=block_shifts.at[block],
            send_sem=hsend_sem.at[hops],
            recv_sem=hrecv_sem.at[hops],
            device_id={"tm": lax.rem(me + hops * group, n)},
            device_id_type=MESH,
        )

    for hops in range(1, blocks):

        @pl.when(block + hops < blocks)
        def _():
            ahead(hops).start()

    for hops in range(1, blocks):

        @pl.when(block > hops)
        def _():
            forward(hops).wait_recv()

        @pl.when(block >= hops)
        def _():
            ahead(hops).wait_recv()

    entering[...] = start[...]

    @pl.when(block > 0)
    def _():
        entering[...] = block_shifts[0, 0:1]

    for k in range(1, blocks - 1):

        @pl.when(block > k)
        def _():
            entering[...] = to_row(
                eye, row_step(eye, block_maps[k], entering[...], block_shifts[k, 0:1])
            )

    entry = entering[...]
    inside = entry
    column = to_column(eye, entry)
    for k in range(group - 1):
        push = shifts[k, 0:1]
        if k % 2:
            column = row_step(eye, maps[k], row, push)
            after = to_row(eye, column)
        else:
            row = column_step(maps[k], column, push)
            after = row
        inside = jnp.where(place == k + 1, after, inside)

    for c in range(count):
        if c:
            column = row_step(eye, heads[c - 1], inside, chunk_ends[c - 1 : c])
        else:
            column = to_column(eye, inside)
        for step in range(STEPS):
            t = c * STEPS + step
            out[t : t + 1] = column_step(prefix[t], column, local[t : t + 1])

    for hops in range(1, blocks):

        @pl.when(jnp.logical_and(block > 0, block + hops < blocks))
        def _():
            forward(hops).wait_send()

        @pl.when(block + hops < blocks)
        def _():
            ahead(hops).wait_send()


VMEM = pl.BlockSpec(memory_space=pltpu.VMEM)
SMEM = pl.BlockSpec(memory_space=pltpu.SMEM)
HBM = pl.BlockSpec(memory_space=pltpu.HBM)
LIMIT = 63 * 1024 * 1024


def shards(n, frames, levels, initial_state, transitions, gain, pixel_mode, pixel_weight):
    group = 4
    while n % group:
        group //= 2
    span = levels.shape[0]
    depth, states = transitions.shape[0], transitions.shape[1]
    pixels = frames.shape[0]
    count = span // STEPS
    square = (states, states)
    dma = pltpu.SemaphoreType.DMA
    return pl.pallas_call(
        functools.partial(fused_kernel, n, group),
        out_shape=jax.ShapeDtypeStruct((span, states), F32),
        in_specs=[SMEM] + [HBM] * 6,
        out_specs=VMEM,
        scratch_shapes=[
            pltpu.VMEM((pixels, n * span), BF16),
            pltpu.VMEM((n * span, pixels), BF16),
            pltpu.VMEM((n, span, pixels), BF16),
            pltpu.VMEM((depth, *square), F32),
            pltpu.VMEM((depth, *square), F32),
            pltpu.VMEM((depth, 2 * states, 2 * states), BF16),
            pltpu.VMEM((span, *square), F32),
            pltpu.VMEM((count, *square), F32),
            pltpu.VMEM((count, *square), F32),
            pltpu.VMEM((2, *square), F32),
            pltpu.VMEM((group, *square), F32),
            pltpu.VMEM(square, F32),
            pltpu.VMEM(square, BF16),
            pltpu.VMEM((n, pixels), jnp.int32),
            pltpu.VMEM((n, pixels), BF16),
            pltpu.VMEM((1, states), F32),
            pltpu.VMEM((n, states, pixels), BF16),
            pltpu.VMEM((span, states), F32),
            pltpu.VMEM((count, states), F32),
            pltpu.VMEM((8, states), F32),
            pltpu.VMEM((group, 8, states), F32),
            pltpu.VMEM((n // group, *square), F32),
            pltpu.VMEM((n // group, 8, states), F32),
            pltpu.VMEM((8, states), F32),
            pltpu.VMEM((1, states), F32),
            dma((6,)),
            dma((2,)),
            dma((n,)),
            dma((n,)),
            dma((group,)),
            dma((group,)),
            dma((group,)),
            dma((group,)),
            dma((n // group,)),
            dma((n // group,)),
            dma((n // group,)),
            dma((n // group,)),
        ],
        compiler_params=pltpu.CompilerParams(
            collective_id=0, has_side_effects=True, vmem_limit_bytes=LIMIT
        ),
        name="filter",
    )(
        levels,
        frames,
        transitions,
        gain,
        pixel_mode.reshape(n, pixels),
        pixel_weight.reshape(n, pixels),
        initial_state.reshape(1, states),
    )


def solution(mesh):
    in_specs = (P("tm", "parts"), P(("parts", "tm")), P("parts"), P(), P(), P(), P())
    out_specs = P(("parts", "tm"), None)
    return jax.shard_map(
        functools.partial(shards, mesh.shape["tm"]),
        mesh=mesh,
        in_specs=in_specs,
        out_specs=out_specs,
        check_vma=False,
    )
```
